512 devices in a mesh: chan: 8 (over z), tm: 64 (over x, y, core).
Axes of the slice: x: 4, y: 8, z: 8, core: 2. Of those that a mesh axis runs over, the one named last changes fastest.
Arguments:
- voltages: bfloat16 [8, 2, 128, 131072], P(None, None, 'chan', 'tm'), may hold values from -100 to 100
- prototype: float32 [64], replicated, may hold values from -5 to 5
- forget: float32 [8], P('chan'), may hold values from 0.5 to 16
Outputs:
- whitened: bfloat16 [8, 256, 131072], P('chan', None, 'tm')
The draws below stay inside these ranges and needn't reach their ends.
All inputs are finite; a program needn't handle non-finite values.
Results may differ from the reference program's by a relative error of at most 0.0071.
Values may be sent and summed in bfloat16 or wider, within the bound.
No kernel may reach another device: no remote copies, remote signals or barrier semaphores. Data moves between devices by JAX's collectives and lax.ppermute only.
A program may use at most 64 MiB of HBM per device.

```python
import math
import jax
import jax.numpy as jnp
from jax import lax

CHANNELS = 8
TAPS = 8
ANTENNAS = 128
SNAP_DEV = 2048
FRAMES = 131072
N_TM = 64


def draw_voltages(key, part):
    keys = jax.random.split(key, 7)
    array_shape = (CHANNELS, 2, ANTENNAS, FRAMES)
    gains = jnp.exp(jax.random.uniform(keys[0], (1, 2, ANTENNAS, 1), jnp.float32, 0.0, 2.302585))
    noise = jax.random.normal(keys[1], array_shape, jnp.float32)
    strength = 0.6
    source_one = jax.random.normal(keys[2], (CHANNELS, 2, 1, FRAMES), jnp.float32)
    source_two = jax.random.normal(keys[3], (CHANNELS, 2, 1, FRAMES), jnp.float32)
    weight_one = jax.random.normal(keys[4], (1, 2, ANTENNAS, 1), jnp.float32)
    weight_two = jax.random.normal(keys[5], (1, 2, ANTENNAS, 1), jnp.float32)
    segment = SNAP_DEV // 4
    envelope = jnp.exp(jax.random.uniform(keys[6], (1, 1, 1, FRAMES // segment), jnp.float32, -1.0, 1.0))
    envelope = jnp.repeat(envelope, segment, axis=3)
    signal = noise + strength * (weight_one * source_one + weight_two * source_two)
    return jnp.clip(envelope * gains * signal, -100.0, 100.0).astype(jnp.bfloat16)


def shard_levels(rng, shape, cuts, smallest, high):
    def one(axis_at, blocks):
        steps = jax.random.uniform(jax.random.fold_in(jax.random.fold_in(rng, 6), axis_at), (blocks,), jnp.float32, smallest / len(cuts), high / len(cuts))
        return jnp.repeat(jnp.exp(steps), shape[axis_at] // blocks).reshape((-1,) + (1,) * (len(shape) - axis_at - 1))

    level = one(*cuts[0])
    for cut in cuts[1:]:
        level = level * one(*cut)
    return level


def bell_draw(rng, dims, scale, limit, held_as=jnp.bfloat16):
    drawn = scale * jax.random.normal(rng, dims, jnp.float32)
    return jnp.clip(drawn, min=-limit, max=limit).astype(held_as)


def setup_inputs(seed: int = 0) -> dict:
    streams_of = jax.random.split(jax.random.key(seed), 4)
    return {
        "voltages": draw_voltages(jax.random.fold_in(streams_of[3], 71), 0),
        "prototype": bell_draw(streams_of[1], (TAPS * CHANNELS,), 0.35, 5.0, jnp.float32),
        "forget": jnp.clip(jnp.exp(math.log(16.0) - 3.465736 * jax.random.uniform(streams_of[2], (CHANNELS,), jnp.float32) ** shard_levels(streams_of[2], (CHANNELS,), ((0, 8),), -0.2, 0.2)), 0.5, 16.0),
    }


def coefficient_table(prototype, tap_count, filter_branches):
    shaped = prototype.reshape(tap_count, filter_branches)
    steps_p = jnp.arange(filter_branches, dtype=jnp.float32)
    phase = 2.0 * math.pi / filter_branches * (steps_p[:, None] * steps_p[None, :])
    cosine = jnp.cos(phase)
    sine = jnp.sin(phase)
    pattern = jnp.stack([jnp.stack([cosine, -sine], -1), jnp.stack([sine, cosine], -1)], axis=1)
    return (shaped[:, :, None, None, None] * pattern[None]).astype(jnp.bfloat16)

def reference(voltages, prototype, forget):
    coef_table = coefficient_table(prototype, TAPS, CHANNELS)
    retain = jnp.exp(-forget / N_TM)
    col_count = 2 * ANTENNAS
    identity_m = jnp.eye(col_count, dtype=jnp.float32)

    def block_step(carry, block_idx):
        tail_rows, prior_gram, prior_count = carry
        start = (block_idx * SNAP_DEV).astype(jnp.int32)
        block = lax.dynamic_slice_in_dim(voltages, start, SNAP_DEV, axis=3)
        extended = jnp.concatenate([tail_rows, block], axis=3).astype(jnp.float32)
        branch_sum = jnp.zeros((CHANNELS, ANTENNAS, 2, SNAP_DEV), jnp.float32)
        for tap_idx in range(TAPS):
            branch_sum = branch_sum + jnp.einsum('pcaf,pckq->kaqf', extended[..., tap_idx:tap_idx + SNAP_DEV], coef_table[tap_idx].astype(jnp.float32))
        spectrum_rows = branch_sum.reshape(CHANNELS, col_count, SNAP_DEV).astype(jnp.bfloat16)
        spec_f = spectrum_rows.astype(jnp.float32)
        gram_now = jnp.einsum('cif,cjf->cij', spec_f, spec_f)
        moment = retain[:, None, None] * prior_gram + gram_now
        weight_sum = retain * prior_count + jnp.float32(SNAP_DEV)
        factor_low = jnp.linalg.cholesky(moment / weight_sum[:, None, None])
        inverse = lax.linalg.triangular_solve(factor_low, jnp.broadcast_to(identity_m, factor_low.shape), left_side=True, lower=True)
        whitened = jnp.einsum('cij,cjf->cif', inverse, spec_f, precision=lax.Precision.HIGHEST).astype(jnp.bfloat16)
        new_tail = block[..., SNAP_DEV - (TAPS - 1):]
        return ((new_tail, moment, weight_sum), whitened)
    init = (jnp.zeros((CHANNELS, 2, ANTENNAS, TAPS - 1), jnp.bfloat16), jnp.zeros((CHANNELS, col_count, col_count), jnp.float32), jnp.zeros((CHANNELS,), jnp.float32))
    _, block_list = lax.scan(block_step, init, jnp.arange(N_TM, dtype=jnp.int32))
    return jnp.transpose(block_list, (1, 2, 0, 3)).reshape(CHANNELS, col_count, N_TM * SNAP_DEV)
```

```python
import math

import jax
import jax.numpy as jnp
from jax import lax
from jax.sharding import PartitionSpec as P


def passed_along(value, axis, steps):
    count = lax.axis_size(axis)
    leading, last = (max(0, -steps), min(count, count - steps))
    return lax.ppermute(value, axis, [(source, source + steps) for source in range(leading, last)])


def coefficient_table(prototype, tap_count, filter_branches):
    shaped = prototype.reshape(tap_count, filter_branches)
    steps_p = jnp.arange(filter_branches, dtype=jnp.float32)
    phase = 2.0 * math.pi / filter_branches * (steps_p[:, None] * steps_p[None, :])
    cosine = jnp.cos(phase)
    sine = jnp.sin(phase)
    pattern = jnp.stack([jnp.stack([cosine, -sine], -1), jnp.stack([sine, cosine], -1)], axis=1)
    return (shaped[:, :, None, None, None] * pattern[None]).astype(jnp.bfloat16)


def running_mean(gram_now, forget, frame_rows):
    count, mine = (lax.axis_size("tm"), lax.axis_index("tm"))
    side = gram_now.shape[-1]
    pieces = gram_now.reshape(count, side * side // (count * 128), 128)
    every = lax.all_to_all(pieces, "tm", split_axis=0, concat_axis=0, tiled=True)
    lag = jnp.arange(count)[:, None] - jnp.arange(count)[None, :]
    decay = jnp.where(lag >= 0, jnp.exp(-forget[0] / count * jnp.maximum(lag, 0).astype(jnp.float32)), 0.0)
    decay = decay / (float(frame_rows) * jnp.sum(decay, axis=1, keepdims=True))
    mean = jnp.einsum("bc,cij->bij", decay, every, precision=lax.Precision.HIGHEST)
    mean = lax.all_to_all(mean, "tm", split_axis=0, concat_axis=0, tiled=True)
    return mean.reshape(gram_now.shape)


def per_device(voltages, prototype, forget):
    filter_branches = voltages.shape[0]
    local_antenna_count = voltages.shape[2]
    frame_rows = voltages.shape[3]
    tap_count = prototype.shape[0] // filter_branches
    coef_table = coefficient_table(prototype, tap_count, filter_branches)
    tail_rows = passed_along(voltages[..., frame_rows - (tap_count - 1) :], "tm", 1)
    extended = jnp.concatenate([tail_rows, voltages], axis=3)
    branch_sum = jnp.zeros((filter_branches, local_antenna_count, 2, frame_rows), jnp.float32)
    for tap_idx in range(tap_count):
        branch_sum = branch_sum + jnp.einsum(
            "pcaf,pckq->kaqf",
            extended[..., tap_idx : tap_idx + frame_rows],
            coef_table[tap_idx],
            preferred_element_type=jnp.float32,
        )
    spectrum_rows = branch_sum.reshape(filter_branches, local_antenna_count * 2, frame_rows).astype(
        jnp.bfloat16
    )
    turned = lax.all_to_all(spectrum_rows, "chan", split_axis=0, concat_axis=1, tiled=True)
    col_count = turned.shape[1]
    gram_now = jnp.einsum("cif,cjf->cij", turned, turned, preferred_element_type=jnp.float32)
    factor_low = jnp.linalg.cholesky(running_mean(gram_now, forget, frame_rows))
    identity_m = jnp.broadcast_to(jnp.eye(col_count, dtype=jnp.float32), factor_low.shape)
    inverse = lax.linalg.triangular_solve(factor_low, identity_m, left_side=True, lower=True)
    whitened = jnp.einsum(
        "cij,cjf->cif", inverse, turned.astype(jnp.float32), precision=lax.Precision.HIGHEST
    )
    return whitened.astype(jnp.bfloat16)


def solution(mesh):
    placed = (P(None, None, "chan", "tm"), P(), P("chan"))
    return jax.shard_map(
        per_device, mesh=mesh, in_specs=placed, out_specs=P("chan", None, "tm"), check_vma=False
    )
```

```python
import math

import jax
import jax.numpy as jnp
import numpy as np
from jax import lax
from jax.experimental import pallas as pl
from jax.experimental.pallas import tpu as pltpu
from jax.sharding import PartitionSpec as P

F32, BF16 = jnp.float32, jnp.bfloat16
LANES = 128
HALO = 128
STEP = 512
GRANT = 12 << 20
PANEL = 16


def passed_along(value, axis):
    count = lax.axis_size(axis)
    return lax.ppermute(value, axis, [(source, source + 1) for source in range(count - 1)])


def turn_pattern(branches, antennas):
    steps = np.arange(branches, dtype=np.float32)
    phase = np.float32(2.0 * math.pi / branches) * (steps[:, None] * steps[None, :])
    cosine, sine = np.cos(phase), np.sin(phase)
    pattern = np.stack([np.stack([cosine, -sine], -1), np.stack([sine, cosine], -1)], axis=1)
    wide = np.einsum("pckq,ab->kaqpcb", pattern, np.eye(antennas, dtype=np.float32))
    return wide.reshape(branches * antennas * 2, branches * 2 * antennas).astype(np.float32)


def filter_body(taps, branches, proto, pattern, tail, before, block, out, weights):
    rows, cols = pattern.shape
    step = pl.program_id(0)

    @pl.when(step == 0)
    def _():
        per_branch = cols // branches
        lane = lax.broadcasted_iota(jnp.int32, (8, cols), 1)
        for tap in range(taps):
            line = jnp.zeros((8, cols), F32)
            for branch in range(branches):
                here = (lane >= branch * per_branch) & (lane < (branch + 1) * per_branch)
                line = jnp.where(here, proto[tap * branches + branch], line)
            weights[tap] = (pattern[...] * line[:1]).astype(BF16)

    first = jnp.where(step == 0, 1, 0)
    halo = jnp.where(first == 1, tail[...], before[...])
    longer = jnp.concatenate([halo, block[...]], axis=1)
    width = block.shape[1]
    total = jnp.zeros((rows, width), F32)
    for tap in range(taps):
        start = HALO - (taps - 1) + tap
        total += jnp.dot(weights[tap], longer[:, start : start + width], preferred_element_type=F32)
    out[...] = total.astype(BF16)


def filter_bank(voltages, prototype):
    branches, parts, antennas, frames = voltages.shape
    taps = prototype.shape[0] // branches
    rows = branches * parts * antennas
    tail = passed_along(voltages[..., frames - HALO :], "tm").reshape(rows, HALO)
    flat = voltages.reshape(rows, frames)
    pattern = jnp.asarray(turn_pattern(branches, antennas))
    per = STEP // HALO
    body = lambda *refs: filter_body(taps, branches, *refs)
    return pl.pallas_call(
        body,
        out_shape=jax.ShapeDtypeStruct((rows, frames), BF16),
        grid=(frames // STEP,),
        in_specs=[
            pl.BlockSpec(memory_space=pltpu.SMEM),
            pl.BlockSpec((rows, rows), lambda i: (0, 0)),
            pl.BlockSpec((rows, HALO), lambda i: (0, 0)),
            pl.BlockSpec((rows, HALO), lambda i: (0, jnp.maximum(i * per - 1, 0))),
            pl.BlockSpec((rows, STEP), lambda i: (0, i)),
        ],
        out_specs=pl.BlockSpec((rows, STEP), lambda i: (0, i)),
        scratch_shapes=[pltpu.VMEM((taps, rows, rows), BF16)],
        compiler_params=pltpu.CompilerParams(vmem_limit_bytes=GRANT),
        name="filter_bank",
    )(prototype, pattern, tail, flat, flat)


def gram_body(x, out):
    for part in range(out.shape[0]):
        some = x[part * LANES : (part + 1) * LANES, :]
        out[part] = lax.dot_general(x[...], some, (((1,), (1,)), ((), ())), preferred_element_type=F32)


def gram(spectra):
    side = spectra.shape[0]
    return pl.pallas_call(
        gram_body,
        out_shape=jax.ShapeDtypeStruct((side // LANES, side, LANES), F32),
        in_specs=[pl.BlockSpec(memory_space=pltpu.VMEM)],
        out_specs=pl.BlockSpec(memory_space=pltpu.VMEM),
        compiler_params=pltpu.CompilerParams(vmem_limit_bytes=GRANT),
        name="gram",
    )(spectra)


def mean_body(frames, count, forget, pieces, out):
    retain = jnp.exp(jnp.full((8, LANES), -forget[0] / count, F32))
    moment = jnp.zeros((8, LANES), F32)
    weight = jnp.zeros((8, LANES), F32)
    for position in range(count):
        moment = retain * moment + pieces[position]
        weight = retain * weight + float(frames)
        out[position] = moment / weight


def running_mean(gram_now, forget, frames):
    count = lax.axis_size("tm")
    pieces = gram_now.reshape(count, -1, LANES)
    every = lax.all_to_all(pieces, "tm", split_axis=0, concat_axis=0, tiled=True)
    mean = pl.pallas_call(
        lambda *refs: mean_body(frames, count, *refs),
        out_shape=jax.ShapeDtypeStruct(every.shape, F32),
        in_specs=[pl.BlockSpec(memory_space=pltpu.SMEM), pl.BlockSpec(memory_space=pltpu.VMEM)],
        out_specs=pl.BlockSpec(memory_space=pltpu.VMEM),
        compiler_params=pltpu.CompilerParams(vmem_limit_bytes=GRANT),
        name="running_mean",
    )(forget, every)
    back = lax.all_to_all(mean, "tm", split_axis=0, concat_axis=0, tiled=True)
    return back.reshape(gram_now.shape)


def in_three(value):
    high = value.astype(BF16)
    rest = value - high.astype(F32)
    middle = rest.astype(BF16)
    return high, middle, (rest - middle.astype(F32)).astype(BF16)


def whiten_body(cov, x, y_hbm, work, inverse, y, y_sem):
    side, frames = x.shape
    half = side // 2
    work[:, :half] = cov[0]
    work[:, half:] = cov[1]
    stores = []

    def whitened(first, last):
        parts = in_three(inverse[first:last, :last])
        for at in range(0, frames, STEP):
            data = x[:last, at : at + STEP]
            total = sum(jnp.dot(part, data, preferred_element_type=F32) for part in parts)
            y[first:last, at : at + STEP] = total.astype(BF16)
            there = (slice(first, last), slice(at, at + STEP))
            store = pltpu.make_async_copy(y.at[there], y_hbm.at[there], y_sem.at[len(stores)])
            store.start()
            stores.append(store)

    lane = lax.broadcasted_iota(jnp.int32, (PANEL, side), 1)
    row = lax.broadcasted_iota(jnp.int32, (PANEL, side), 0)
    sub = lax.broadcasted_iota(jnp.int32, (PANEL, LANES), 0)
    panels = side // PANEL
    for panel in range(panels):
        at = panel * PANEL
        final = panel == panels - 1
        tall = PANEL if final else 2 * PANEL
        inside = (lane >= at) & (lane < at + PANEL)
        base = at // LANES * LANES
        near = work[at : at + tall, base : base + LANES]
        cols = [
            jnp.broadcast_to(near[:, at - base + c : at - base + c + 1], (tall, LANES))
            for c in range(PANEL)
        ]
        rows = jnp.where(inside, (lane - at == row).astype(F32), work[at : at + PANEL, :])
        if not final:
            later = jnp.where(inside, 0.0, work[at + PANEL : at + tall, :])
        scale = jnp.zeros((PANEL, LANES), F32)
        for j in range(PANEL):
            pivot = 1.0 / jnp.broadcast_to(cols[j][j : j + 1, :], (8, LANES))
            pivot = jnp.concatenate([pivot] * (tall // 8), 0)
            scale = jnp.where(sub == j, pivot[:PANEL], scale)
            if final and j == PANEL - 1:
                break
            factor = cols[j] * pivot
            for c in range(j + 1, PANEL):
                cols[c] = cols[c] - factor * jnp.broadcast_to(cols[j][c : c + 1, :], (tall, LANES))
            source = jnp.broadcast_to(rows[j : j + 1, :], (PANEL, side))
            if j < PANEL - 1:
                below = jnp.where(sub > j, factor[:PANEL], 0.0)
                rows = rows - jnp.concatenate([below] * (side // LANES), 1) * source
            if not final:
                later = later - jnp.concatenate([factor[PANEL:]] * (side // LANES), 1) * source
        scale = jnp.concatenate([scale] * (side // LANES), 1)
        inverse[at : at + PANEL, :] = jnp.where(lane < at + PANEL, rows * jnp.sqrt(scale), 0.0)
        if not final:
            work[at + PANEL : at + tall, :] = later
        if panel < panels - 2:
            rest = at + 2 * PANEL
            cut = rest // LANES * LANES
            a, b, c = in_three((rows * scale)[:, cut:])
            d, e, f = in_three(rows)
            update = lax.dot_general(
                jnp.concatenate([a, a, b, b, a, c], 0),
                jnp.concatenate([d, e, d, e, f, d], 0),
                (((0,), (0,)), ((), ())),
                preferred_element_type=F32,
            )
            wide = lax.broadcasted_iota(jnp.int32, (side - rest, side), 1)
            held = jnp.where((wide >= at) & (wide < at + PANEL), 0.0, work[rest:, :])
            work[rest:, :] = held - update[rest - cut :]
        if panel == panels // 2 - 1:
            whitened(0, half)
    whitened(half, side)
    for store in stores:
        store.wait()


def whiten(cov, spectra):
    side, frames = spectra.shape
    chunks = 2 * (frames // STEP)
    return pl.pallas_call(
        whiten_body,
        out_shape=jax.ShapeDtypeStruct(spectra.shape, BF16),
        in_specs=[pl.BlockSpec(memory_space=pltpu.VMEM)] * 2,
        out_specs=pl.BlockSpec(memory_space=pl.ANY),
        scratch_shapes=[
            pltpu.VMEM((side, side), F32),
            pltpu.VMEM((side, side), F32),
            pltpu.VMEM((side, frames), BF16),
            pltpu.SemaphoreType.DMA((chunks,)),
        ],
        compiler_params=pltpu.CompilerParams(vmem_limit_bytes=GRANT),
        name="whiten",
    )(cov, spectra)


def per_device(voltages, prototype, forget):
    frames = voltages.shape[3]
    channels = lax.axis_size("chan")
    spectra = filter_bank(voltages, prototype).reshape(channels, -1, frames)
    turned = lax.all_to_all(spectra, "chan", split_axis=0, concat_axis=0, tiled=True)
    turned = turned.reshape(-1, frames)
    mean = running_mean(gram(turned), forget, frames)
    return whiten(mean, turned)[None]


def solution(mesh):
    placed = (P(None, None, "chan", "tm"), P(), P("chan"))
    return jax.shard_map(
        per_device, mesh=mesh, in_specs=placed, out_specs=P("chan", None, "tm"), check_vma=False
    )
```

```python
import math

import jax
import jax.numpy as jnp
import numpy as np
from jax import lax
from jax.experimental import pallas as pl
from jax.experimental.pallas import tpu as pltpu
from jax.sharding import PartitionSpec as P

F32, BF16 = jnp.float32, jnp.bfloat16
LANES = 128
LOWEST = float(np.finfo(np.float32).min)
HALO = 128
STEP = 512
GRANT = 12 << 20
PANEL = 16


def passed_along(value, axis):
    count = lax.axis_size(axis)
    return lax.ppermute(value, axis, [(source, source + 1) for source in range(count - 1)])


def turn_pattern(branches, antennas):
    steps = np.arange(branches, dtype=np.float32)
    phase = np.float32(2.0 * math.pi / branches) * (steps[:, None] * steps[None, :])
    cosine, sine = np.cos(phase), np.sin(phase)
    pattern = np.stack([np.stack([cosine, -sine], -1), np.stack([sine, cosine], -1)], axis=1)
    lines = pattern.transpose(2, 3, 0, 1).reshape(branches * 2, branches * 2)
    return np.repeat(lines, antennas, axis=1).astype(np.float32)


def tap_weights(proto, pattern, weights, branches, antennas):
    cols = pattern.shape[1]
    taps = weights.shape[1] // cols
    per_branch = cols // branches
    lane = lax.broadcasted_iota(jnp.int32, (8, cols), 1)
    lines = []
    for tap in range(taps):
        line = jnp.zeros((8, cols), F32)
        for branch in range(branches):
            here = (lane >= branch * per_branch) & (lane < (branch + 1) * per_branch)
            line = jnp.where(here, proto[tap * branches + branch], line)
        lines.append(jnp.broadcast_to(line[:1], (2 * antennas, cols)))
    shape = (2 * antennas, cols)
    part = lax.broadcasted_iota(jnp.int32, shape, 0) & 1
    antenna = lax.broadcasted_iota(jnp.int32, shape, 0) >> 1
    same = antenna == (lax.broadcasted_iota(jnp.int32, shape, 1) & (antennas - 1))
    for channel in range(branches):
        real = jnp.broadcast_to(pattern[2 * channel : 2 * channel + 1, :], shape)
        imag = jnp.broadcast_to(pattern[2 * channel + 1 : 2 * channel + 2, :], shape)
        turn = jnp.where(same, jnp.where(part == 0, real, imag), 0.0)
        rows = slice(channel * 2 * antennas, (channel + 1) * 2 * antennas)
        for tap in range(taps):
            weights[rows, tap * cols : (tap + 1) * cols] = (turn * lines[tap]).astype(BF16)


def filtered(weights, longer, width):
    rows = longer.shape[0]
    taps = weights.shape[1] // rows
    first = longer.shape[1] - width - (taps - 1)
    total = jnp.zeros((weights.shape[0], width), F32)
    for tap in range(taps):
        data = longer[:, first + tap : first + tap + width]
        total += jnp.dot(weights[:, tap * rows : (tap + 1) * rows], data, preferred_element_type=F32)
    return total.astype(BF16)


def filter_body(branches, antennas, count, proto, forget, pattern, x_hbm, out, weights, start, retain, x, sems):
    rows, frames = x_hbm.shape
    fetches = []
    for at in range(0, frames, STEP):
        there = (slice(None), slice(at, at + STEP))
        fetches.append(pltpu.make_async_copy(x_hbm.at[there], x.at[there], sems.at[at // STEP]))
        fetches[-1].start()
    tap_weights(proto, pattern, weights, branches, antennas)
    for at in range(0, frames, STEP):
        fetches[at // STEP].wait()
        halo = x[:, at - HALO : at] if at else jnp.zeros((rows, HALO), BF16)
        longer = jnp.concatenate([halo, x[:, at : at + STEP]], axis=1)
        out[:, at : at + STEP] = filtered(weights, longer, STEP)
    start[...] = x[:, :HALO]
    retain[...] = jnp.exp(jnp.full(retain.shape, -forget[0] / count, F32))


def filter_bank(flat, prototype, forget, branches, antennas):
    rows, frames = flat.shape
    taps = prototype.shape[0] // branches
    pattern = jnp.asarray(turn_pattern(branches, antennas))
    count = lax.axis_size("tm")
    smem = pl.BlockSpec(memory_space=pltpu.SMEM)
    vmem = pl.BlockSpec(memory_space=pltpu.VMEM)
    return pl.pallas_call(
        lambda *refs: filter_body(branches, antennas, count, *refs),
        out_shape=(
            jax.ShapeDtypeStruct((rows, frames), BF16),
            jax.ShapeDtypeStruct((rows, rows * taps), BF16),
            jax.ShapeDtypeStruct((rows, HALO), BF16),
            jax.ShapeDtypeStruct((8, LANES), F32),
        ),
        in_specs=[smem, smem, vmem, pl.BlockSpec(memory_space=pltpu.HBM)],
        out_specs=(vmem,) * 4,
        scratch_shapes=[
            pltpu.VMEM((rows, frames), BF16),
            pltpu.SemaphoreType.DMA((frames // STEP,)),
        ],
        compiler_params=pltpu.CompilerParams(vmem_limit_bytes=GRANT),
        cost_estimate=pl.CostEstimate(
            flops=2 * taps * rows * rows * frames, bytes_accessed=4 * rows * frames, transcendentals=0
        ),
        name="filter_bank",
    )(prototype, forget, pattern, pltpu.with_memory_space_constraint(flat, pltpu.HBM))


def head_body(tail, start, weights, alone, out):
    longer = jnp.concatenate([tail[...], start[...]], axis=1)
    out[...] = filtered(weights, longer, HALO)


def with_history(alone, weights, start, tail):
    rows, frames = alone.shape
    vmem = pl.BlockSpec(memory_space=pltpu.VMEM)
    head = pl.BlockSpec((rows, HALO), lambda i: (0, 0))
    return pl.pallas_call(
        head_body,
        out_shape=jax.ShapeDtypeStruct((rows, frames), BF16),
        grid=(1,),
        in_specs=[vmem, vmem, vmem, pl.BlockSpec(memory_space=pl.ANY)],
        out_specs=head,
        input_output_aliases={3: 0},
        compiler_params=pltpu.CompilerParams(vmem_limit_bytes=GRANT),
        name="with_history",
    )(tail, start, weights, alone)


def gram_body(x, out):
    for part in range(out.shape[0]):
        some = x[part * LANES : (part + 1) * LANES, :]
        out[part] = lax.dot_general(x[...], some, (((1,), (1,)), ((), ())), preferred_element_type=F32)


def gram(spectra):
    side = spectra.shape[0]
    vmem = pl.BlockSpec(memory_space=pltpu.VMEM)
    return pl.pallas_call(
        gram_body,
        out_shape=jax.ShapeDtypeStruct((side // LANES, side, LANES), F32),
        in_specs=[vmem],
        out_specs=vmem,
        compiler_params=pltpu.CompilerParams(vmem_limit_bytes=GRANT),
        name="gram",
    )(spectra)


def mean_body(frames, retained, pieces, out):
    retain = retained[...]
    moment = jnp.zeros((8, LANES), F32)
    weight = jnp.zeros((8, LANES), F32)
    for position in range(pieces.shape[0]):
        moment = retain * moment + pieces[position]
        weight = retain * weight + float(frames)
        out[position] = moment / weight


def running_mean(gram_now, retained, frames):
    count = lax.axis_size("tm")
    pieces = gram_now.reshape(count, -1, LANES)
    every = lax.all_to_all(pieces, "tm", split_axis=0, concat_axis=0, tiled=True)
    mean = pl.pallas_call(
        lambda *refs: mean_body(frames, *refs),
        out_shape=jax.ShapeDtypeStruct(every.shape, F32),
        in_specs=[pl.BlockSpec(memory_space=pltpu.VMEM)] * 2,
        out_specs=pl.BlockSpec(memory_space=pltpu.VMEM),
        compiler_params=pltpu.CompilerParams(vmem_limit_bytes=GRANT),
        name="running_mean",
    )(retained, every)
    back = lax.all_to_all(mean, "tm", split_axis=0, concat_axis=0, tiled=True)
    return back.reshape(gram_now.shape)


def in_three(value):
    high = value.astype(BF16)
    rest = value - high.astype(F32)
    middle = rest.astype(BF16)
    return high, middle, (rest - middle.astype(F32)).astype(BF16)


def whiten_body(cov, x, y_hbm, work, inverse, y, y_sem):
    side, frames = x.shape
    half = side // 2
    work[:, :half] = cov[0]
    work[:, half:] = cov[1]
    stores = []

    def whitened(first, last):
        parts = in_three(inverse[first:last, :last])
        for at in range(0, frames, STEP):
            data = x[:last, at : at + STEP]
            total = sum(jnp.dot(part, data, preferred_element_type=F32) for part in parts)
            y[first:last, at : at + STEP] = total.astype(BF16)
            there = (slice(first, last), slice(at, at + STEP))
            store = pltpu.make_async_copy(y.at[there], y_hbm.at[there], y_sem.at[len(stores)])
            store.start()
            stores.append(store)

    lane = lax.broadcasted_iota(jnp.int32, (PANEL, side), 1)
    row = lax.broadcasted_iota(jnp.int32, (PANEL, side), 0)
    sub = lax.broadcasted_iota(jnp.int32, (8, LANES), 0)
    panels = side // PANEL
    own = PANEL // 8

    def eights(value):
        return [value[r : r + 8] for r in range(0, value.shape[0], 8)]

    def line(tile, at):
        return jnp.broadcast_to(tile[at : at + 1, :], tile.shape)

    def across(tile):
        return jnp.concatenate([tile] * (side // LANES), 1)

    for panel in range(panels):
        at = panel * PANEL
        final = panel == panels - 1
        tall = PANEL if final else 2 * PANEL
        inside = (lane >= at) & (lane < at + PANEL)
        base = at // LANES * LANES
        near = work[at : at + tall, base : base + LANES]
        cols = []
        for c in range(PANEL):
            spread = jnp.broadcast_to(near[:, at - base + c : at - base + c + 1], (tall, LANES))
            cols.append(eights(jnp.maximum(spread, LOWEST)))
        rows = eights(jnp.where(inside, (lane - at == row).astype(F32), work[at : at + PANEL, :]))
        later = []
        if not final:
            later = eights(jnp.where(inside, 0.0, work[at + PANEL : at + tall, :]))
        scale = [jnp.zeros((8, LANES), F32)] * own
        for j in range(PANEL):
            top = j // 8
            pivot = 1.0 / line(cols[j][top], j % 8)
            scale[top] = jnp.where(sub == j % 8, pivot, scale[top])
            factor = [None if r < top else tile * pivot for r, tile in enumerate(cols[j])]
            for c in range(j + 1, PANEL):
                shared = line(cols[j][c // 8], c % 8)
                for r in range(c // 8, tall // 8):
                    cols[c][r] = cols[c][r] - factor[r] * shared
            source = line(rows[top], j % 8)
            for r in range(top, own):
                below = jnp.where(sub > j % 8, factor[r], 0.0) if r == top else factor[r]
                rows[r] = rows[r] - across(below) * source
            for r in range(len(later)):
                later[r] = later[r] - across(factor[own + r]) * source
        rows = jnp.concatenate(rows, 0)
        scale = jnp.concatenate(scale, 0)
        scale = jnp.concatenate([scale] * (side // LANES), 1)
        inverse[at : at + PANEL, :] = jnp.where(lane < at + PANEL, rows * jnp.sqrt(scale), 0.0)
        if not final:
            work[at + PANEL : at + tall, :] = jnp.concatenate(later, 0)
        if panel < panels - 2:
            rest = at + 2 * PANEL
            cut = rest // LANES * LANES
            a, b, c = in_three((rows * scale)[:, cut:])
            d, e, f = in_three(rows)
            update = lax.dot_general(
                jnp.concatenate([a, a, b, b, a, c], 0),
                jnp.concatenate([d, e, d, e, f, d], 0),
                (((0,), (0,)), ((), ())),
                preferred_element_type=F32,
            )
            wide = lax.broadcasted_iota(jnp.int32, (side - rest, side), 1)
            held = jnp.where((wide >= at) & (wide < at + PANEL), 0.0, work[rest:, :])
            work[rest:, :] = held - update[rest - cut :]
        if (panel + 1) % (panels // 4) == 0 and panel > panels // 4:
            done = at + PANEL
            whitened(0 if done == half else done - side // 4, done)
    for store in stores:
        store.wait()


def whiten(cov, spectra):
    side, frames = spectra.shape
    chunks = 3 * (frames // STEP)
    return pl.pallas_call(
        whiten_body,
        out_shape=jax.ShapeDtypeStruct(spectra.shape, BF16),
        in_specs=[pl.BlockSpec(memory_space=pltpu.VMEM)] * 2,
        out_specs=pl.BlockSpec(memory_space=pl.ANY),
        scratch_shapes=[
            pltpu.VMEM((side, side), F32),
            pltpu.VMEM((side, side), F32),
            pltpu.VMEM((side, frames), BF16),
            pltpu.SemaphoreType.DMA((chunks,)),
        ],
        compiler_params=pltpu.CompilerParams(vmem_limit_bytes=GRANT),
        name="whiten",
    )(cov, spectra)


def per_device(voltages, prototype, forget):
    branches, parts, antennas, frames = voltages.shape
    flat = voltages.reshape(-1, frames)
    tail = passed_along(flat[:, frames - HALO :], "tm")
    alone, weights, start, retained = filter_bank(flat, prototype, forget, branches, antennas)
    spectra = with_history(alone, weights, start, tail).reshape(branches, -1, frames)
    turned = lax.all_to_all(spectra, "chan", split_axis=0, concat_axis=0, tiled=True)
    turned = turned.reshape(-1, frames)
    mean = running_mean(gram(turned), retained, frames)
    return whiten(mean, turned)[None]


def solution(mesh):
    placed = (P(None, None, "chan", "tm"), P(), P("chan"))
    return jax.shard_map(
        per_device, mesh=mesh, in_specs=placed, out_specs=P("chan", None, "tm"), check_vma=False
    )
```

```python
import math

import jax
import jax.numpy as jnp
import numpy as np
from jax import lax
from jax.experimental import pallas as pl
from jax.experimental.pallas import tpu as pltpu
from jax.sharding import PartitionSpec as P

F32, BF16 = jnp.float32, jnp.bfloat16
LANES = 128
LOWEST = float(np.finfo(np.float32).min)
HALO = 128
STEP = 512
GRANT = 12 << 20
PANEL = 16


def passed_along(value, axis):
    count = lax.axis_size(axis)
    return lax.ppermute(value, axis, [(source, source + 1) for source in range(count - 1)])


def turn_pattern(branches, antennas):
    steps = np.arange(branches, dtype=np.float32)
    phase = np.float32(2.0 * math.pi / branches) * (steps[:, None] * steps[None, :])
    cosine, sine = np.cos(phase), np.sin(phase)
    pattern = np.stack([np.stack([cosine, -sine], -1), np.stack([sine, cosine], -1)], axis=1)
    lines = pattern.transpose(2, 3, 0, 1).reshape(branches * 2, branches * 2)
    return np.repeat(lines, antennas, axis=1).astype(np.float32)


def tap_weights(proto, pattern, weights, branches, antennas):
    cols = pattern.shape[1]
    taps = weights.shape[1] // cols
    per_branch = cols // branches
    lane = lax.broadcasted_iota(jnp.int32, (8, cols), 1)
    lines = []
    for tap in range(taps):
        line = jnp.zeros((8, cols), F32)
        for branch in range(branches):
            here = (lane >= branch * per_branch) & (lane < (branch + 1) * per_branch)
            line = jnp.where(here, proto[tap * branches + branch], line)
        lines.append(jnp.broadcast_to(line[:1], (2 * antennas, cols)))
    shape = (2 * antennas, cols)
    part = lax.broadcasted_iota(jnp.int32, shape, 0) & 1
    antenna = lax.broadcasted_iota(jnp.int32, shape, 0) >> 1
    same = antenna == (lax.broadcasted_iota(jnp.int32, shape, 1) & (antennas - 1))
    for channel in range(branches):
        real = jnp.broadcast_to(pattern[2 * channel : 2 * channel + 1, :], shape)
        imag = jnp.broadcast_to(pattern[2 * channel + 1 : 2 * channel + 2, :], shape)
        turn = jnp.where(same, jnp.where(part == 0, real, imag), 0.0)
        rows = slice(channel * 2 * antennas, (channel + 1) * 2 * antennas)
        for tap in range(taps):
            weights[rows, tap * cols : (tap + 1) * cols] = (turn * lines[tap]).astype(BF16)


def filtered(weights, longer, width):
    rows = longer.shape[0]
    taps = weights.shape[1] // rows
    first = longer.shape[1] - width - (taps - 1)
    total = jnp.zeros((weights.shape[0], width), F32)
    for tap in range(taps):
        data = longer[:, first + tap : first + tap + width]
        total += jnp.dot(weights[:, tap * rows : (tap + 1) * rows], data, preferred_element_type=F32)
    return total.astype(BF16)


def filter_body(
    branches, antennas, count, proto_hbm, forget, pattern, x_hbm,
    out, weights, start, retain, x, proto, sems, proto_sem,
):
    rows, frames = x_hbm.shape
    small = pltpu.make_async_copy(proto_hbm, proto, proto_sem)
    small.start()
    fetches = []
    for at in range(0, frames, STEP):
        there = (slice(None), slice(at, at + STEP))
        fetches.append(pltpu.make_async_copy(x_hbm.at[there], x.at[there], sems.at[at // STEP]))
        fetches[-1].start()
    small.wait()
    tap_weights(proto, pattern, weights, branches, antennas)
    for fetch in fetches:
        fetch.wait()
    for at in range(0, frames, STEP):
        halo = x[:, at - HALO : at] if at else jnp.zeros((rows, HALO), BF16)
        longer = jnp.concatenate([halo, x[:, at : at + STEP]], axis=1)
        out[:, at : at + STEP] = filtered(weights, longer, STEP)
    start[...] = x[:, :HALO]
    retain[...] = jnp.exp(jnp.full(retain.shape, -forget[0] / count, F32))


def filter_bank(flat, prototype, forget, branches, antennas):
    rows, frames = flat.shape
    taps = prototype.shape[0] // branches
    pattern = jnp.asarray(turn_pattern(branches, antennas))
    count = lax.axis_size("tm")
    hbm = pl.BlockSpec(memory_space=pltpu.HBM)
    vmem = pl.BlockSpec(memory_space=pltpu.VMEM)
    stay = lambda value: pltpu.with_memory_space_constraint(value, pltpu.HBM)
    return pl.pallas_call(
        lambda *refs: filter_body(branches, antennas, count, *refs),
        out_shape=(
            jax.ShapeDtypeStruct((rows, frames), BF16),
            jax.ShapeDtypeStruct((rows, rows * taps), BF16),
            jax.ShapeDtypeStruct((rows, HALO), BF16),
            jax.ShapeDtypeStruct((8, LANES), F32),
        ),
        in_specs=[hbm, pl.BlockSpec(memory_space=pltpu.SMEM), vmem, hbm],
        out_specs=(vmem,) * 4,
        scratch_shapes=[
            pltpu.VMEM((rows, frames), BF16),
            pltpu.SMEM(prototype.shape, F32),
            pltpu.SemaphoreType.DMA((frames // STEP,)),
            pltpu.SemaphoreType.DMA,
        ],
        compiler_params=pltpu.CompilerParams(vmem_limit_bytes=GRANT),
        cost_estimate=pl.CostEstimate(
            flops=2 * taps * rows * rows * frames, bytes_accessed=4 * rows * frames, transcendentals=0
        ),
        name="filter_bank",
    )(stay(prototype), forget, pattern, stay(flat))


def head_body(tail, start, weights, alone, out):
    longer = jnp.concatenate([tail[...], start[...]], axis=1)
    out[...] = filtered(weights, longer, HALO)


def with_history(alone, weights, start, tail):
    rows, frames = alone.shape
    vmem = pl.BlockSpec(memory_space=pltpu.VMEM)
    head = pl.BlockSpec((rows, HALO), lambda i: (0, 0))
    return pl.pallas_call(
        head_body,
        out_shape=jax.ShapeDtypeStruct((rows, frames), BF16),
        grid=(1,),
        in_specs=[vmem, vmem, vmem, pl.BlockSpec(memory_space=pl.ANY)],
        out_specs=head,
        input_output_aliases={3: 0},
        compiler_params=pltpu.CompilerParams(vmem_limit_bytes=GRANT),
        name="with_history",
    )(tail, start, weights, alone)


def gram_body(x, out):
    for part in range(out.shape[0]):
        some = x[part * LANES : (part + 1) * LANES, :]
        out[part] = lax.dot_general(x[...], some, (((1,), (1,)), ((), ())), preferred_element_type=F32)


def gram(spectra):
    side = spectra.shape[0]
    vmem = pl.BlockSpec(memory_space=pltpu.VMEM)
    return pl.pallas_call(
        gram_body,
        out_shape=jax.ShapeDtypeStruct((side // LANES, side, LANES), F32),
        in_specs=[vmem],
        out_specs=vmem,
        compiler_params=pltpu.CompilerParams(vmem_limit_bytes=GRANT),
        name="gram",
    )(spectra)


def mean_body(frames, retained, pieces, out):
    retain = retained[...]
    moment = jnp.zeros((8, LANES), F32)
    weight = jnp.zeros((8, LANES), F32)
    for position in range(pieces.shape[0]):
        moment = retain * moment + pieces[position]
        weight = retain * weight + float(frames)
        out[position] = moment / weight


def running_mean(gram_now, retained, frames):
    count = lax.axis_size("tm")
    pieces = gram_now.reshape(count, -1, LANES)
    every = lax.all_to_all(pieces, "tm", split_axis=0, concat_axis=0, tiled=True)
    mean = pl.pallas_call(
        lambda *refs: mean_body(frames, *refs),
        out_shape=jax.ShapeDtypeStruct(every.shape, F32),
        in_specs=[pl.BlockSpec(memory_space=pltpu.VMEM)] * 2,
        out_specs=pl.BlockSpec(memory_space=pltpu.VMEM),
        compiler_params=pltpu.CompilerParams(vmem_limit_bytes=GRANT),
        name="running_mean",
    )(retained, every)
    back = lax.all_to_all(mean, "tm", split_axis=0, concat_axis=0, tiled=True)
    return back.reshape(gram_now.shape)


def in_three(value):
    high = value.astype(BF16)
    rest = value - high.astype(F32)
    middle = rest.astype(BF16)
    return high, middle, (rest - middle.astype(F32)).astype(BF16)


def whiten_body(cov, x, y_hbm, work, inverse, y, y_sem):
    side, frames = x.shape
    half = side // 2
    work[:, :half] = cov[0]
    work[:, half:] = cov[1]
    stores = []

    def whitened(first, last):
        parts = in_three(inverse[first:last, :last])
        for at in range(0, frames, STEP):
            data = x[:last, at : at + STEP]
            total = sum(jnp.dot(part, data, preferred_element_type=F32) for part in parts)
            y[first:last, at : at + STEP] = total.astype(BF16)
            there = (slice(first, last), slice(at, at + STEP))
            store = pltpu.make_async_copy(y.at[there], y_hbm.at[there], y_sem.at[len(stores)])
            store.start()
            stores.append(store)

    lane = lax.broadcasted_iota(jnp.int32, (PANEL, side), 1)
    row = lax.broadcasted_iota(jnp.int32, (PANEL, side), 0)
    sub = lax.broadcasted_iota(jnp.int32, (8, LANES), 0)
    panels = side // PANEL
    own = PANEL // 8

    def eights(value):
        return [value[r : r + 8] for r in range(0, value.shape[0], 8)]

    def line(tile, at):
        return jnp.broadcast_to(tile[at : at + 1, :], tile.shape)

    def across(tile):
        return jnp.concatenate([tile] * (side // LANES), 1)

    for panel in range(panels):
        at = panel * PANEL
        final = panel == panels - 1
        tall = PANEL if final else 2 * PANEL
        inside = (lane >= at) & (lane < at + PANEL)
        base = at // LANES * LANES
        near = work[at : at + tall, base : base + LANES]
        cols = []
        for c in range(PANEL):
            spread = jnp.broadcast_to(near[:, at - base + c : at - base + c + 1], (tall, LANES))
            cols.append(eights(jnp.maximum(spread, LOWEST)))
        rows = eights(jnp.where(inside, (lane - at == row).astype(F32), work[at : at + PANEL, :]))
        later = []
        if not final:
            later = eights(jnp.where(inside, 0.0, work[at + PANEL : at + tall, :]))
        scale = [jnp.zeros((8, LANES), F32)] * own
        for j in range(PANEL):
            top = j // 8
            pivot = 1.0 / line(cols[j][top], j % 8)
            scale[top] = jnp.where(sub == j % 8, pivot, scale[top])
            factor = [None if r < top else tile * pivot for r, tile in enumerate(cols[j])]
            for c in range(j + 1, PANEL):
                shared = line(cols[j][c // 8], c % 8)
                for r in range(c // 8, tall // 8):
                    cols[c][r] = cols[c][r] - factor[r] * shared
            source = line(rows[top], j % 8)
            for r in range(top, own):
                below = jnp.where(sub > j % 8, factor[r], 0.0) if r == top else factor[r]
                rows[r] = rows[r] - across(below) * source
            for r in range(len(later)):
                later[r] = later[r] - across(factor[own + r]) * source
        rows = jnp.concatenate(rows, 0)
        scale = jnp.concatenate(scale, 0)
        scale = jnp.concatenate([scale] * (side // LANES), 1)
        inverse[at : at + PANEL, :] = jnp.where(lane < at + PANEL, rows * jnp.sqrt(scale), 0.0)
        if not final:
            work[at + PANEL : at + tall, :] = jnp.concatenate(later, 0)
        if panel < panels - 2:
            rest = at + 2 * PANEL
            cut = rest // LANES * LANES
            a, b, c = in_three((rows * scale)[:, cut:])
            d, e, f = in_three(rows)
            update = lax.dot_general(
                jnp.concatenate([a, a, b, b, a, c], 0),
                jnp.concatenate([d, e, d, e, f, d], 0),
                (((0,), (0,)), ((), ())),
                preferred_element_type=F32,
            )
            wide = lax.broadcasted_iota(jnp.int32, (side - rest, side), 1)
            held = jnp.where((wide >= at) & (wide < at + PANEL), 0.0, work[rest:, :])
            work[rest:, :] = held - update[rest - cut :]
        if (panel + 1) % (panels // 4) == 0 and panel > panels // 4:
            done = at + PANEL
            whitened(0 if done == half else done - side // 4, done)
    for store in stores:
        store.wait()


def whiten(cov, spectra):
    side, frames = spectra.shape
    chunks = 3 * (frames // STEP)
    return pl.pallas_call(
        whiten_body,
        out_shape=jax.ShapeDtypeStruct(spectra.shape, BF16),
        in_specs=[pl.BlockSpec(memory_space=pltpu.VMEM)] * 2,
        out_specs=pl.BlockSpec(memory_space=pl.ANY),
        scratch_shapes=[
            pltpu.VMEM((side, side), F32),
            pltpu.VMEM((side, side), F32),
            pltpu.VMEM((side, frames), BF16),
            pltpu.SemaphoreType.DMA((chunks,)),
        ],
        compiler_params=pltpu.CompilerParams(vmem_limit_bytes=GRANT),
        name="whiten",
    )(cov, spectra)


def per_device(voltages, prototype, forget):
    branches, parts, antennas, frames = voltages.shape
    flat = voltages.reshape(-1, frames)
    tail = passed_along(flat[:, frames - HALO :], "tm")
    alone, weights, start, retained = filter_bank(flat, prototype, forget, branches, antennas)
    spectra = with_history(alone, weights, start, tail).reshape(branches, -1, frames)
    turned = lax.all_to_all(spectra, "chan", split_axis=0, concat_axis=0, tiled=True)
    turned = turned.reshape(-1, frames)
    mean = running_mean(gram(turned), retained, frames)
    return whiten(mean, turned)[None]


def solution(mesh):
    placed = (P(None, None, "chan", "tm"), P(), P("chan"))
    return jax.shard_map(
        per_device, mesh=mesh, in_specs=placed, out_specs=P("chan", None, "tm"), check_vma=False
    )
```

```python
import math

import jax
import jax.numpy as jnp
import numpy as np
from jax import lax
from jax.experimental import pallas as pl
from jax.experimental.pallas import tpu as pltpu
from jax.sharding import PartitionSpec as P

F32, BF16 = jnp.float32, jnp.bfloat16
LANES = 128
LOWEST = float(np.finfo(np.float32).min)
HALO = 128
STEP = 512
GRANT = 12 << 20
PANEL = 16


def passed_along(value, axis):
    count = lax.axis_size(axis)
    return lax.ppermute(value, axis, [(source, source + 1) for source in range(count - 1)])


def turn_pattern(branches, antennas):
    steps = np.arange(branches, dtype=np.float32)
    phase = np.float32(2.0 * math.pi / branches) * (steps[:, None] * steps[None, :])
    cosine, sine = np.cos(phase), np.sin(phase)
    pattern = np.stack([np.stack([cosine, -sine], -1), np.stack([sine, cosine], -1)], axis=1)
    lines = pattern.transpose(2, 3, 0, 1).reshape(branches * 2, branches * 2)
    return np.repeat(lines, antennas, axis=1).astype(np.float32)


def tap_weights(proto, pattern, weights, branches, antennas):
    cols = pattern.shape[1]
    taps = weights.shape[1] // cols
    per_branch = cols // branches
    lane = lax.broadcasted_iota(jnp.int32, (8, cols), 1)
    lines = []
    for tap in range(taps):
        line = jnp.zeros((8, cols), F32)
        for branch in range(branches):
            here = (lane >= branch * per_branch) & (lane < (branch + 1) * per_branch)
            line = jnp.where(here, proto[tap * branches + branch], line)
        lines.append(jnp.broadcast_to(line[:1], (2 * antennas, cols)))
    shape = (2 * antennas, cols)
    part = lax.broadcasted_iota(jnp.int32, shape, 0) & 1
    antenna = lax.broadcasted_iota(jnp.int32, shape, 0) >> 1
    same = antenna == (lax.broadcasted_iota(jnp.int32, shape, 1) & (antennas - 1))
    for channel in range(branches):
        real = jnp.broadcast_to(pattern[2 * channel : 2 * channel + 1, :], shape)
        imag = jnp.broadcast_to(pattern[2 * channel + 1 : 2 * channel + 2, :], shape)
        turn = jnp.where(same, jnp.where(part == 0, real, imag), 0.0)
        rows = slice(channel * 2 * antennas, (channel + 1) * 2 * antennas)
        for tap in range(taps):
            weights[rows, tap * cols : (tap + 1) * cols] = (turn * lines[tap]).astype(BF16)


def filtered(weights, longer, width):
    rows = longer.shape[0]
    taps = weights.shape[1] // rows
    first = longer.shape[1] - width - (taps - 1)
    total = jnp.zeros((weights.shape[0], width), F32)
    for tap in range(taps):
        data = longer[:, first + tap : first + tap + width]
        total += jnp.dot(weights[:, tap * rows : (tap + 1) * rows], data, preferred_element_type=F32)
    return total.astype(BF16)


def filter_body(
    branches, antennas, count, proto_hbm, forget, pattern, x_hbm,
    out, weights, start, retain, x, proto, sems, proto_sem,
):
    rows, frames = x_hbm.shape
    small = pltpu.make_async_copy(proto_hbm, proto, proto_sem)
    small.start()
    fetches = []
    for at in range(0, frames, STEP):
        there = (slice(None), slice(at, at + STEP))
        fetches.append(pltpu.make_async_copy(x_hbm.at[there], x.at[there], sems.at[at // STEP]))
        fetches[-1].start()
    small.wait()
    tap_weights(proto, pattern, weights, branches, antennas)
    for fetch in fetches:
        fetch.wait()
    for at in range(0, frames, STEP):
        halo = x[:, at - HALO : at] if at else jnp.zeros((rows, HALO), BF16)
        longer = jnp.concatenate([halo, x[:, at : at + STEP]], axis=1)
        out[:, at : at + STEP] = filtered(weights, longer, STEP)
    start[...] = x[:, :HALO]
    retain[...] = jnp.exp(jnp.full(retain.shape, -forget[0] / count, F32))


def filter_bank(flat, prototype, forget, branches, antennas):
    rows, frames = flat.shape
    taps = prototype.shape[0] // branches
    pattern = jnp.asarray(turn_pattern(branches, antennas))
    count = lax.axis_size("tm")
    hbm = pl.BlockSpec(memory_space=pltpu.HBM)
    vmem = pl.BlockSpec(memory_space=pltpu.VMEM)
    stay = lambda value: pltpu.with_memory_space_constraint(value, pltpu.HBM)
    return pl.pallas_call(
        lambda *refs: filter_body(branches, antennas, count, *refs),
        out_shape=(
            jax.ShapeDtypeStruct((rows, frames), BF16),
            jax.ShapeDtypeStruct((rows, rows * taps), BF16),
            jax.ShapeDtypeStruct((rows, HALO), BF16),
            jax.ShapeDtypeStruct((8, LANES), F32),
        ),
        in_specs=[hbm, pl.BlockSpec(memory_space=pltpu.SMEM), vmem, hbm],
        out_specs=(vmem,) * 4,
        scratch_shapes=[
            pltpu.VMEM((rows, frames), BF16),
            pltpu.SMEM(prototype.shape, F32),
            pltpu.SemaphoreType.DMA((frames // STEP,)),
            pltpu.SemaphoreType.DMA,
        ],
        compiler_params=pltpu.CompilerParams(vmem_limit_bytes=GRANT),
        cost_estimate=pl.CostEstimate(
            flops=2 * taps * rows * rows * frames, bytes_accessed=4 * rows * frames, transcendentals=0
        ),
        name="filter_bank",
    )(stay(prototype), forget, pattern, stay(flat))


def head_body(tail, start, weights, alone, out):
    longer = jnp.concatenate([tail[...], start[...]], axis=1)
    out[...] = filtered(weights, longer, HALO)


def with_history(alone, weights, start, tail):
    rows, frames = alone.shape
    vmem = pl.BlockSpec(memory_space=pltpu.VMEM)
    head = pl.BlockSpec((rows, HALO), lambda i: (0, 0))
    return pl.pallas_call(
        head_body,
        out_shape=jax.ShapeDtypeStruct((rows, frames), BF16),
        grid=(1,),
        in_specs=[vmem, vmem, vmem, pl.BlockSpec(memory_space=pl.ANY)],
        out_specs=head,
        input_output_aliases={3: 0},
        compiler_params=pltpu.CompilerParams(vmem_limit_bytes=GRANT),
        name="with_history",
    )(tail, start, weights, alone)


def gram_body(x, out):
    dims = (((1,), (1,)), ((), ()))
    low, high = x[:LANES, :], x[LANES:, :]
    first = lax.dot_general(low, low, dims, preferred_element_type=F32)
    second = lax.dot_general(high, high, dims, preferred_element_type=F32)
    row = lax.broadcasted_iota(jnp.int32, (LANES, LANES), 0)
    col = lax.broadcasted_iota(jnp.int32, (LANES, LANES), 1)
    out[:LANES, :] = lax.dot_general(high, low, dims, preferred_element_type=F32)
    out[LANES : 2 * LANES, :] = jnp.where(col <= row, first, second)
    diagonal = jnp.sum(jnp.where(col == row, second, 0.0), axis=0, keepdims=True)
    out[2 * LANES :, :] = jnp.broadcast_to(diagonal, (out.shape[0] - 2 * LANES, LANES))


def gram(spectra, count):
    rows = -(-(2 * LANES + 1) // count) * count
    vmem = pl.BlockSpec(memory_space=pltpu.VMEM)
    return pl.pallas_call(
        gram_body,
        out_shape=jax.ShapeDtypeStruct((rows, LANES), F32),
        in_specs=[vmem],
        out_specs=vmem,
        compiler_params=pltpu.CompilerParams(vmem_limit_bytes=GRANT),
        name="gram",
    )(spectra)


def mean_body(frames, count, retained, pieces, out):
    each = pieces.shape[0] // count
    retain = retained[:each, :]
    moment = jnp.zeros((each, LANES), F32)
    weight = jnp.zeros((each, LANES), F32)
    for position in range(count):
        here = slice(position * each, (position + 1) * each)
        moment = retain * moment + pieces[here, :]
        weight = retain * weight + float(frames)
        out[here, :] = moment / weight


def exchanged(packed):
    count = lax.axis_size("tm")
    pieces = packed.reshape(count, -1, 1, LANES)
    return lax.all_to_all(pieces, "tm", split_axis=0, concat_axis=0, tiled=True).reshape(packed.shape)


def running_mean(gram_now, retained, frames):
    every = exchanged(gram_now)
    count = lax.axis_size("tm")
    mean = pl.pallas_call(
        lambda *refs: mean_body(frames, count, *refs),
        out_shape=jax.ShapeDtypeStruct(every.shape, F32),
        in_specs=[pl.BlockSpec(memory_space=pltpu.VMEM)] * 2,
        out_specs=pl.BlockSpec(memory_space=pltpu.VMEM),
        compiler_params=pltpu.CompilerParams(vmem_limit_bytes=GRANT),
        name="running_mean",
    )(retained, every)
    return exchanged(mean)


def in_three(value):
    high = value.astype(BF16)
    rest = value - high.astype(F32)
    middle = rest.astype(BF16)
    return high, middle, (rest - middle.astype(F32)).astype(BF16)


def whiten_body(cov, x, y_hbm, work, inverse, y, y_sem):
    side, frames = x.shape
    half = side // 2
    packed = cov[half : 2 * half, :]
    square_row = lax.broadcasted_iota(jnp.int32, (half, half), 0)
    square_col = lax.broadcasted_iota(jnp.int32, (half, half), 1)
    turned = packed.T
    corner = jnp.where(square_col > square_row, packed, turned)
    work[:half, :half] = jnp.where(square_col <= square_row, packed, turned)
    work[half:, :half] = cov[:half, :]
    work[:half, half:] = cov[:half, :].T
    work[half:, half:] = jnp.where(square_col == square_row, cov[2 * half : 2 * half + 1, :], corner)
    stores = []

    def whitened(first, last):
        parts = in_three(inverse[first:last, :last])
        for at in range(0, frames, STEP):
            data = x[:last, at : at + STEP]
            total = sum(jnp.dot(part, data, preferred_element_type=F32) for part in parts)
            y[first:last, at : at + STEP] = total.astype(BF16)
            there = (slice(first, last), slice(at, at + STEP))
            store = pltpu.make_async_copy(y.at[there], y_hbm.at[there], y_sem.at[len(stores)])
            store.start()
            stores.append(store)

    lane = lax.broadcasted_iota(jnp.int32, (PANEL, side), 1)
    row = lax.broadcasted_iota(jnp.int32, (PANEL, side), 0)
    sub = lax.broadcasted_iota(jnp.int32, (8, LANES), 0)
    panels = side // PANEL
    own = PANEL // 8

    def eights(value):
        return [value[r : r + 8] for r in range(0, value.shape[0], 8)]

    def line(tile, at):
        return jnp.broadcast_to(tile[at : at + 1, :], tile.shape)

    def across(tile):
        return jnp.concatenate([tile] * (side // LANES), 1)

    for panel in range(panels):
        at = panel * PANEL
        final = panel == panels - 1
        tall = PANEL if final else 2 * PANEL
        inside = (lane >= at) & (lane < at + PANEL)
        base = at // LANES * LANES
        near = work[at : at + tall, base : base + LANES]
        cols = []
        for c in range(PANEL):
            spread = jnp.broadcast_to(near[:, at - base + c : at - base + c + 1], (tall, LANES))
            cols.append(eights(jnp.maximum(spread, LOWEST)))
        rows = eights(jnp.where(inside, (lane - at == row).astype(F32), work[at : at + PANEL, :]))
        later = []
        if not final:
            later = eights(jnp.where(inside, 0.0, work[at + PANEL : at + tall, :]))
        scale = [jnp.zeros((8, LANES), F32)] * own
        for j in range(PANEL):
            top = j // 8
            pivot = 1.0 / line(cols[j][top], j % 8)
            scale[top] = jnp.where(sub == j % 8, pivot, scale[top])
            factor = [None if r < top else tile * pivot for r, tile in enumerate(cols[j])]
            for c in range(j + 1, PANEL):
                shared = line(cols[j][c // 8], c % 8)
                for r in range(c // 8, tall // 8):
                    cols[c][r] = cols[c][r] - factor[r] * shared
            source = line(rows[top], j % 8)
            for r in range(top, own):
                below = jnp.where(sub > j % 8, factor[r], 0.0) if r == top else factor[r]
                rows[r] = rows[r] - across(below) * source
            for r in range(len(later)):
                later[r] = later[r] - across(factor[own + r]) * source
        rows = jnp.concatenate(rows, 0)
        scale = jnp.concatenate(scale, 0)
        scale = jnp.concatenate([scale] * (side // LANES), 1)
        inverse[at : at + PANEL, :] = jnp.where(lane < at + PANEL, rows * jnp.sqrt(scale), 0.0)
        if not final:
            work[at + PANEL : at + tall, :] = jnp.concatenate(later, 0)
        if panel < panels - 2:
            rest = at + 2 * PANEL
            cut = rest // LANES * LANES
            a, b, c = in_three((rows * scale)[:, cut:])
            d, e, f = in_three(rows)
            update = lax.dot_general(
                jnp.concatenate([a, a, b, b, a, c], 0),
                jnp.concatenate([d, e, d, e, f, d], 0),
                (((0,), (0,)), ((), ())),
                preferred_element_type=F32,
            )
            wide = lax.broadcasted_iota(jnp.int32, (side - rest, side), 1)
            held = jnp.where((wide >= at) & (wide < at + PANEL), 0.0, work[rest:, :])
            work[rest:, :] = held - update[rest - cut :]
        if (panel + 1) % (panels // 4) == 0 and panel > panels // 4:
            done = at + PANEL
            whitened(0 if done == half else done - side // 4, done)
    for store in stores:
        store.wait()


def whiten(cov, spectra):
    side, frames = spectra.shape
    chunks = 3 * (frames // STEP)
    return pl.pallas_call(
        whiten_body,
        out_shape=jax.ShapeDtypeStruct(spectra.shape, BF16),
        in_specs=[pl.BlockSpec(memory_space=pltpu.VMEM)] * 2,
        out_specs=pl.BlockSpec(memory_space=pl.ANY),
        scratch_shapes=[
            pltpu.VMEM((side, side), F32),
            pltpu.VMEM((side, side), F32),
            pltpu.VMEM((side, frames), BF16),
            pltpu.SemaphoreType.DMA((chunks,)),
        ],
        compiler_params=pltpu.CompilerParams(vmem_limit_bytes=GRANT),
        name="whiten",
    )(cov, spectra)


def per_device(voltages, prototype, forget):
    branches, parts, antennas, frames = voltages.shape
    flat = voltages.reshape(-1, frames)
    tail = passed_along(flat[:, frames - HALO :], "tm")
    alone, weights, start, retained = filter_bank(flat, prototype, forget, branches, antennas)
    spectra = with_history(alone, weights, start, tail).reshape(branches, -1, frames)
    turned = lax.all_to_all(spectra, "chan", split_axis=0, concat_axis=0, tiled=True)
    turned = turned.reshape(-1, frames)
    mean = running_mean(gram(turned, lax.axis_size("tm")), retained, frames)
    return whiten(mean, turned)[None]


def solution(mesh):
    placed = (P(None, None, "chan", "tm"), P(), P("chan"))
    return jax.shard_map(
        per_device, mesh=mesh, in_specs=placed, out_specs=P("chan", None, "tm"), check_vma=False
    )
```

```python
import math

import jax
import jax.numpy as jnp
import numpy as np
from jax import lax
from jax.experimental import pallas as pl
from jax.experimental.pallas import tpu as pltpu
from jax.sharding import PartitionSpec as P

F32, BF16 = jnp.float32, jnp.bfloat16
LANES = 128
LOWEST = float(np.finfo(np.float32).min)
HALO = 128
STEP = 512
GRANT = 12 << 20
PANEL = 16


def passed_along(value, axis):
    count = lax.axis_size(axis)
    return lax.ppermute(value, axis, [(source, source + 1) for source in range(count - 1)])


def turn_pattern(branches, antennas):
    steps = np.arange(branches, dtype=np.float32)
    phase = np.float32(2.0 * math.pi / branches) * (steps[:, None] * steps[None, :])
    cosine, sine = np.cos(phase), np.sin(phase)
    pattern = np.stack([np.stack([cosine, -sine], -1), np.stack([sine, cosine], -1)], axis=1)
    lines = pattern.transpose(2, 3, 0, 1).reshape(branches * 2, branches * 2)
    return np.repeat(lines, antennas, axis=1).astype(np.float32)


def tap_weights(proto, pattern, weights, branches, antennas):
    cols = pattern.shape[1]
    taps = weights.shape[1] // cols
    per_branch = cols // branches
    lane = lax.broadcasted_iota(jnp.int32, (8, cols), 1)
    lines = []
    for tap in range(taps):
        line = jnp.zeros((8, cols), F32)
        for branch in range(branches):
            here = (lane >= branch * per_branch) & (lane < (branch + 1) * per_branch)
            line = jnp.where(here, proto[tap * branches + branch], line)
        lines.append(jnp.broadcast_to(line[:1], (2 * antennas, cols)))
    shape = (2 * antennas, cols)
    part = lax.broadcasted_iota(jnp.int32, shape, 0) & 1
    antenna = lax.broadcasted_iota(jnp.int32, shape, 0) >> 1
    same = antenna == (lax.broadcasted_iota(jnp.int32, shape, 1) & (antennas - 1))
    for channel in range(branches):
        real = jnp.broadcast_to(pattern[2 * channel : 2 * channel + 1, :], shape)
        imag = jnp.broadcast_to(pattern[2 * channel + 1 : 2 * channel + 2, :], shape)
        turn = jnp.where(same, jnp.where(part == 0, real, imag), 0.0)
        rows = slice(channel * 2 * antennas, (channel + 1) * 2 * antennas)
        for tap in range(taps):
            weights[rows, tap * cols : (tap + 1) * cols] = (turn * lines[tap]).astype(BF16)


def filtered(weights, longer, width):
    rows = longer.shape[0]
    taps = weights.shape[1] // rows
    first = longer.shape[1] - width - (taps - 1)
    total = jnp.zeros((weights.shape[0], width), F32)
    for tap in range(taps):
        data = longer[:, first + tap : first + tap + width]
        total += jnp.dot(weights[:, tap * rows : (tap + 1) * rows], data, preferred_element_type=F32)
    return total.astype(BF16)


def filter_body(
    branches, antennas, count, proto_hbm, forget, pattern, x_hbm,
    out, weights, start, retain, x, proto, sems, proto_sem,
):
    rows, frames = x_hbm.shape
    small = pltpu.make_async_copy(proto_hbm, proto, proto_sem)
    small.start()
    fetches = []
    for at in range(0, frames, STEP):
        there = (slice(None), slice(at, at + STEP))
        fetches.append(pltpu.make_async_copy(x_hbm.at[there], x.at[there], sems.at[at // STEP]))
        fetches[-1].start()
    small.wait()
    tap_weights(proto, pattern, weights, branches, antennas)
    for fetch in fetches[:2]:
        fetch.wait()
    for at in range(0, frames, STEP):
        if at == 2 * STEP:
            for fetch in fetches[2:]:
                fetch.wait()
        first = max(at, HALO)
        longer = x[:, first - HALO : at + STEP]
        out[:, first : at + STEP] = filtered(weights, longer, at + STEP - first)
    start[...] = x[:, :HALO]
    retain[...] = jnp.exp(jnp.full(retain.shape, -forget[0] / count, F32))


def filter_bank(flat, prototype, forget, branches, antennas):
    rows, frames = flat.shape
    taps = prototype.shape[0] // branches
    pattern = jnp.asarray(turn_pattern(branches, antennas))
    count = lax.axis_size("tm")
    hbm = pl.BlockSpec(memory_space=pltpu.HBM)
    vmem = pl.BlockSpec(memory_space=pltpu.VMEM)
    stay = lambda value: pltpu.with_memory_space_constraint(value, pltpu.HBM)
    return pl.pallas_call(
        lambda *refs: filter_body(branches, antennas, count, *refs),
        out_shape=(
            jax.ShapeDtypeStruct((rows, frames), BF16),
            jax.ShapeDtypeStruct((rows, rows * taps), BF16),
            jax.ShapeDtypeStruct((rows, HALO), BF16),
            jax.ShapeDtypeStruct((8, LANES), F32),
        ),
        in_specs=[hbm, pl.BlockSpec(memory_space=pltpu.SMEM), vmem, hbm],
        out_specs=(vmem,) * 4,
        scratch_shapes=[
            pltpu.VMEM((rows, frames), BF16),
            pltpu.SMEM(prototype.shape, F32),
            pltpu.SemaphoreType.DMA((frames // STEP,)),
            pltpu.SemaphoreType.DMA,
        ],
        compiler_params=pltpu.CompilerParams(vmem_limit_bytes=GRANT),
        cost_estimate=pl.CostEstimate(
            flops=2 * taps * rows * rows * frames, bytes_accessed=4 * rows * frames, transcendentals=0
        ),
        name="filter_bank",
    )(stay(prototype), forget, pattern, stay(flat))


def head_body(tail, start, weights, alone, out):
    longer = jnp.concatenate([tail[...], start[...]], axis=1)
    out[...] = filtered(weights, longer, HALO)


def with_history(alone, weights, start, tail):
    rows, frames = alone.shape
    vmem = pl.BlockSpec(memory_space=pltpu.VMEM)
    head = pl.BlockSpec((rows, HALO), lambda i: (0, 0))
    return pl.pallas_call(
        head_body,
        out_shape=jax.ShapeDtypeStruct((rows, frames), BF16),
        grid=(1,),
        in_specs=[vmem, vmem, vmem, pl.BlockSpec(memory_space=pl.ANY)],
        out_specs=head,
        input_output_aliases={3: 0},
        compiler_params=pltpu.CompilerParams(vmem_limit_bytes=GRANT),
        name="with_history",
    )(tail, start, weights, alone)


def gram_body(x, out):
    dims = (((1,), (1,)), ((), ()))
    low, high = x[:LANES, :], x[LANES:, :]
    first = lax.dot_general(low, low, dims, preferred_element_type=F32)
    second = lax.dot_general(high, high, dims, preferred_element_type=F32)
    row = lax.broadcasted_iota(jnp.int32, (LANES, LANES), 0)
    col = lax.broadcasted_iota(jnp.int32, (LANES, LANES), 1)
    out[:LANES, :] = lax.dot_general(high, low, dims, preferred_element_type=F32)
    out[LANES : 2 * LANES, :] = jnp.where(col <= row, first, second)
    diagonal = jnp.sum(jnp.where(col == row, second, 0.0), axis=0, keepdims=True)
    out[2 * LANES :, :] = jnp.broadcast_to(diagonal, (out.shape[0] - 2 * LANES, LANES))


def gram(spectra, count):
    rows = -(-(2 * LANES + 1) // count) * count
    vmem = pl.BlockSpec(memory_space=pltpu.VMEM)
    return pl.pallas_call(
        gram_body,
        out_shape=jax.ShapeDtypeStruct((rows, LANES), F32),
        in_specs=[vmem],
        out_specs=vmem,
        compiler_params=pltpu.CompilerParams(vmem_limit_bytes=GRANT),
        name="gram",
    )(spectra)


def mean_body(frames, count, retained, pieces, out):
    each = pieces.shape[0] // count
    retain = retained[:each, :]
    moment = jnp.zeros((each, LANES), F32)
    weight = jnp.zeros((each, LANES), F32)
    for position in range(count):
        here = slice(position * each, (position + 1) * each)
        moment = retain * moment + pieces[here, :]
        weight = retain * weight + float(frames)
        out[here, :] = moment / weight


def exchanged(packed):
    count = lax.axis_size("tm")
    pieces = packed.reshape(count, -1, 1, LANES)
    return lax.all_to_all(pieces, "tm", split_axis=0, concat_axis=0, tiled=True).reshape(packed.shape)


def running_mean(gram_now, retained, frames):
    every = exchanged(gram_now)
    count = lax.axis_size("tm")
    mean = pl.pallas_call(
        lambda *refs: mean_body(frames, count, *refs),
        out_shape=jax.ShapeDtypeStruct(every.shape, F32),
        in_specs=[pl.BlockSpec(memory_space=pltpu.VMEM)] * 2,
        out_specs=pl.BlockSpec(memory_space=pltpu.VMEM),
        compiler_params=pltpu.CompilerParams(vmem_limit_bytes=GRANT),
        name="running_mean",
    )(retained, every)
    return exchanged(mean)


def in_three(value):
    high = value.astype(BF16)
    rest = value - high.astype(F32)
    middle = rest.astype(BF16)
    return high, middle, (rest - middle.astype(F32)).astype(BF16)


def whiten_body(cov, x, y_hbm, work, inverse, y, y_sem):
    side, frames = x.shape
    half = side // 2
    packed = cov[half : 2 * half, :]
    square_row = lax.broadcasted_iota(jnp.int32, (half, half), 0)
    square_col = lax.broadcasted_iota(jnp.int32, (half, half), 1)
    turned = packed.T
    corner = jnp.where(square_col > square_row, packed, turned)
    work[:half, :half] = jnp.where(square_col <= square_row, packed, turned)
    work[half:, :half] = cov[:half, :]
    work[:half, half:] = cov[:half, :].T
    work[half:, half:] = jnp.where(square_col == square_row, cov[2 * half : 2 * half + 1, :], corner)
    stores = []

    def whitened(first, last):
        parts = in_three(inverse[first:last, :last])
        for at in range(0, frames, STEP):
            data = x[:last, at : at + STEP]
            total = sum(jnp.dot(part, data, preferred_element_type=F32) for part in parts)
            y[first:last, at : at + STEP] = total.astype(BF16)
            there = (slice(first, last), slice(at, at + STEP))
            store = pltpu.make_async_copy(y.at[there], y_hbm.at[there], y_sem.at[len(stores)])
            store.start()
            stores.append(store)

    lane = lax.broadcasted_iota(jnp.int32, (PANEL, side), 1)
    row = lax.broadcasted_iota(jnp.int32, (PANEL, side), 0)
    sub = lax.broadcasted_iota(jnp.int32, (8, LANES), 0)
    panels = side // PANEL
    own = PANEL // 8

    def eights(value):
        return [value[r : r + 8] for r in range(0, value.shape[0], 8)]

    def line(tile, at):
        return jnp.broadcast_to(tile[at : at + 1, :], tile.shape)

    def across(tile):
        return jnp.concatenate([tile] * (side // LANES), 1)

    for panel in range(panels):
        at = panel * PANEL
        final = panel == panels - 1
        tall = PANEL if final else 2 * PANEL
        inside = (lane >= at) & (lane < at + PANEL)
        base = at // LANES * LANES
        near = work[at : at + tall, base : base + LANES]
        cols = []
        for c in range(PANEL):
            spread = jnp.broadcast_to(near[:, at - base + c : at - base + c + 1], (tall, LANES))
            cols.append(eights(jnp.maximum(spread, LOWEST)))
        rows = eights(jnp.where(inside, (lane - at == row).astype(F32), work[at : at + PANEL, :]))
        later = []
        if not final:
            later = eights(jnp.where(inside, 0.0, work[at + PANEL : at + tall, :]))
        scale = [jnp.zeros((8, LANES), F32)] * own
        for j in range(PANEL):
            top = j // 8
            pivot = 1.0 / line(cols[j][top], j % 8)
            scale[top] = jnp.where(sub == j % 8, pivot, scale[top])
            factor = [None if r < top else tile * pivot for r, tile in enumerate(cols[j])]
            for c in range(j + 1, PANEL):
                shared = line(cols[j][c // 8], c % 8)
                for r in range(c // 8, tall // 8):
                    cols[c][r] = cols[c][r] - factor[r] * shared
            source = line(rows[top], j % 8)
            for r in range(top, own):
                below = jnp.where(sub > j % 8, factor[r], 0.0) if r == top else factor[r]
                rows[r] = rows[r] - across(below) * source
            for r in range(len(later)):
                later[r] = later[r] - across(factor[own + r]) * source
        rows = jnp.concatenate(rows, 0)
        scale = jnp.concatenate(scale, 0)
        scale = jnp.concatenate([scale] * (side // LANES), 1)
        inverse[at : at + PANEL, :] = jnp.where(lane < at + PANEL, rows * jnp.sqrt(scale), 0.0)
        if not final:
            work[at + PANEL : at + tall, :] = jnp.concatenate(later, 0)
        if panel < panels - 2:
            rest = at + 2 * PANEL
            cut = rest // LANES * LANES
            a, b, c = in_three((rows * scale)[:, cut:])
            d, e, f = in_three(rows)
            update = lax.dot_general(
                jnp.concatenate([a, a, b, b, a, c], 0),
                jnp.concatenate([d, e, d, e, f, d], 0),
                (((0,), (0,)), ((), ())),
                preferred_element_type=F32,
            )
            wide = lax.broadcasted_iota(jnp.int32, (side - rest, side), 1)
            held = jnp.where((wide >= at) & (wide < at + PANEL), 0.0, work[rest:, :])
            work[rest:, :] = held - update[rest - cut :]
        if (panel + 1) % (panels // 4) == 0 and panel > panels // 4:
            done = at + PANEL
            whitened(0 if done == half else done - side // 4, done)
    for store in stores:
        store.wait()


def whiten(cov, spectra):
    side, frames = spectra.shape
    chunks = 3 * (frames // STEP)
    return pl.pallas_call(
        whiten_body,
        out_shape=jax.ShapeDtypeStruct(spectra.shape, BF16),
        in_specs=[pl.BlockSpec(memory_space=pltpu.VMEM)] * 2,
        out_specs=pl.BlockSpec(memory_space=pl.ANY),
        scratch_shapes=[
            pltpu.VMEM((side, side), F32),
            pltpu.VMEM((side, side), F32),
            pltpu.VMEM((side, frames), BF16),
            pltpu.SemaphoreType.DMA((chunks,)),
        ],
        compiler_params=pltpu.CompilerParams(vmem_limit_bytes=GRANT),
        name="whiten",
    )(cov, spectra)


def per_device(voltages, prototype, forget):
    branches, parts, antennas, frames = voltages.shape
    flat = voltages.reshape(-1, frames)
    tail = passed_along(flat[:, frames - HALO :], "tm")
    alone, weights, start, retained = filter_bank(flat, prototype, forget, branches, antennas)
    spectra = with_history(alone, weights, start, tail).reshape(branches, -1, frames)
    turned = lax.all_to_all(spectra, "chan", split_axis=0, concat_axis=0, tiled=True)
    turned = turned.reshape(-1, frames)
    mean = running_mean(gram(turned, lax.axis_size("tm")), retained, frames)
    return whiten(mean, turned)[None]


def solution(mesh):
    placed = (P(None, None, "chan", "tm"), P(), P("chan"))
    return jax.shard_map(
        per_device, mesh=mesh, in_specs=placed, out_specs=P("chan", None, "tm"), check_vma=False
    )
```
